32 devices in a mesh: pix: 8 (over z, x), beam: 4 (over y, core).
Axes of the slice: x: 2, y: 2, z: 4, core: 2. Of those that a mesh axis runs over, the one named last changes fastest.
Arguments:
- sketch: bfloat16 [512, 128, 256], P('beam', 'pix'), may hold values from -6 to 6
- gains: bfloat16 [512, 32, 128, 128], P('pix', 'beam'), may hold values from -0.09375 to 0.09375
- coverage: int32 [512, 32], P('pix', 'beam'), may hold values from 0 to 127
Outputs:
- basis: float32 [512, 128, 256], P('beam', 'pix')
- factor: float32 [256, 256], replicated
The draws below stay inside these ranges and needn't reach their ends.
Inputs may be any that keep to these rules, and one draw needn't show every extreme that they name: `coverage`: entries name beam blocks within the slot's group of 128 blocks; a block may be named by several slots.
All inputs are finite; a program needn't handle non-finite values.
Results may differ from the reference program's by a relative error of at most 0.0011.
Values may be sent and summed in bfloat16 or wider, within the bound.
No kernel may reach another device: no remote copies, remote signals or barrier semaphores. Data moves between devices by JAX's collectives and lax.ppermute only.
A program may use at most 192 MiB of HBM per device.

```python
import math
import jax
import jax.numpy as jnp
import numpy as np
from jax import lax

BLOCK = 128
BEAMS = 65536
K = 256
SLOTS_G = 8
BLK = 512
BLK_DEV = 128
TILES = 512
SLOTS = 32


def touch_ends(array, own_key, smallest, top_value):
    longest = array.shape.index(max(array.shape))
    spots = []
    for shift in (0, 1):
        where = [jax.random.randint(jax.random.fold_in(own_key, axis), (), 0, length) for axis, length in enumerate(array.shape)]
        where[longest] = (where[longest] + shift) % array.shape[longest]
        spots.append(tuple(where))
    return array.at[spots[0]].set(smallest).at[spots[1]].set(top_value)


def block_scale(stream_key, shape, cuts, least, top_value):
    level, own = 1.0, jax.random.fold_in(stream_key, 6)
    for dim, parts in cuts:
        draws = jnp.exp(jax.random.uniform(jax.random.fold_in(own, dim), (parts,), jnp.float32, least / len(cuts), top_value / len(cuts)))
        level = level * jnp.repeat(draws, shape[dim] // parts).reshape([-1 if axis == dim else 1 for axis in range(len(shape))])
    return level


def rank_bounds(amount, slope):
    weights = [(1 << 20) // math.isqrt(rank ** slope) + 1 for rank in range(1, amount + 1)]
    width = 1 + sum(weights) // (1 << 30)
    return np.cumsum(np.array([max(1, weight // width) for weight in weights]))


def ranked(key, shape, number_of, lean):
    listing = rank_bounds(number_of, lean)
    pick = jax.random.randint(jax.random.fold_in(key, 1), shape, 0, int(listing[number_of - 1]))
    standing = jnp.searchsorted(jnp.asarray(listing, jnp.int32), pick, side="right")
    return jax.random.permutation(jax.random.fold_in(key, 2), number_of)[standing].astype(jnp.int32)


def bell_draw(key, extent, deviation, bound, cuts=(), held_as=jnp.bfloat16):
    loudness = block_scale(key, extent, cuts, -0.22, 0.18) if cuts else 1.0
    drawn = jax.random.normal(key, extent, jnp.float32) * deviation * loudness
    return jnp.minimum(jnp.maximum(drawn, -bound), bound).astype(held_as)


def setup_inputs(seed: int = 0) -> dict:
    splits = jax.random.split(jax.random.key(seed), 4)
    sketch = bell_draw(splits[0], (BLK, BLOCK, K), 1.0, 6.0, ((0, 4), (1, 8)))
    gains = bell_draw(splits[1], (TILES, SLOTS, BLOCK, BLOCK), (SLOTS * BLOCK) ** -0.5, 0.09375, ((0, 8), (1, 4)))
    coverage = touch_ends(ranked(splits[2], (TILES, SLOTS), BLK_DEV, 1), jax.random.fold_in(splits[2], 3), 0, BLK_DEV - 1).astype(jnp.int32)
    return {"sketch": sketch, "gains": gains, "coverage": coverage}


def reference(sketch, gains, coverage):
    group_base = jnp.arange(SLOTS, dtype=jnp.int32) // SLOTS_G * BLK_DEV
    global_ids = (coverage + group_base[None, :]).astype(jnp.int32)

    def pixel_pass(args):
        tile_gains, tile_ids = args
        picked = sketch[tile_ids].astype(jnp.float32)
        return jnp.einsum('sab,sbk->ak', tile_gains.astype(jnp.float32), picked)
    pixel_sketch = lax.map(pixel_pass, (gains, global_ids))
    rounded = pixel_sketch.astype(jnp.bfloat16)

    def beam_pass(total, args):
        tile_gains, tile_ids, tile_rows = args
        contrib = jnp.einsum('sab,ak->sbk', tile_gains.astype(jnp.float32), tile_rows.astype(jnp.float32))
        return (total.at[tile_ids].add(contrib), None)
    start = jnp.zeros((BLK, BLOCK, K), jnp.float32)
    range_rows, _ = lax.scan(beam_pass, start, (gains, global_ids, rounded))
    flat = range_rows.reshape(BEAMS, K)
    gram = jnp.dot(flat.T.astype(jnp.float32), flat.astype(jnp.float32), precision=lax.Precision.HIGHEST, preferred_element_type=jnp.float32)
    lower = jnp.linalg.cholesky(gram)
    solved = jax.scipy.linalg.solve_triangular(lower, flat.T, lower=True).T
    scale = jnp.sqrt(jnp.float32(BEAMS))
    return ((solved * scale).reshape(BLK, BLOCK, K), lower.T / scale)
```

```python
import functools
import math

import jax
import jax.numpy as jnp
import numpy as np
from jax import lax
from jax.experimental import pallas as pl
from jax.experimental.pallas import tpu as pltpu
from jax.sharding import PartitionSpec as P

BF16, F32, S16 = jnp.bfloat16, jnp.float32, jnp.int16
HIGHEST = lax.Precision.HIGHEST
SUB = 16
STEPS = 256.0
TOP = 32760.0
LEAST = 1e-30
PIECES = 2
GROUPS = 2


def cost(flops, nbytes):
    return pl.CostEstimate(flops=int(flops), bytes_accessed=int(nbytes), transcendentals=0)


def encode(v, out, groups):
    n, sub, width = v.shape
    g = v.reshape(groups, n // groups * sub, width)
    peak = jnp.maximum(jnp.max(jnp.abs(g), axis=1), LEAST)
    power = jnp.ceil(jnp.log2(peak) * STEPS)
    gain = jnp.exp2(power * (-1.0 / STEPS)) * TOP
    q = jnp.round(g * gain[:, None, :]).reshape(n, sub, width)
    out[0:n] = q.astype(jnp.int32).astype(S16)
    if groups < sub:
        power = jnp.concatenate([power, jnp.zeros((sub - groups, width), F32)], axis=0)
    out[n] = power.astype(jnp.int32).astype(S16)


def decode(msg, groups):
    n = msg.shape[0] - 1
    sub, width = msg.shape[1:]
    power = msg[n].astype(jnp.int32).astype(F32)[0:groups]
    gain = jnp.exp2(power * (1.0 / STEPS)) * (1.0 / TOP)
    q = msg[0:n].astype(jnp.int32).astype(F32).reshape(groups, n // groups * sub, width)
    return (q * gain[:, None, :]).reshape(n, sub, width)


def half_start(meta, other):
    return 1 - meta[0] if other else meta[0]


def pixel_kernel(ids, meta, *refs, other, spans, rows, slots, per_step, steps):
    count = len(spans)
    gains_ref, sources = refs[0], refs[1 : 1 + count]
    out_ref, held, sems = refs[1 + count :]
    step = pl.program_id(0)

    @pl.when(step == 0)
    def _():
        copies = []
        for m in range(count):
            first, number, offset = spans[m]
            start = 0 if offset is None else pl.multiple_of(meta[1 + offset] * rows, rows)
            target = held.at[pl.ds(first, number), pl.ds(start, rows), :]
            copies.append(pltpu.make_async_copy(sources[m], target, sems.at[m]))
        for c in copies:
            c.start()
        for c in copies:
            c.wait()

    base = (half_start(meta, other) * steps + step) * per_step * slots
    for i in range(per_step):
        acc = None
        for j in range(0, slots, 2):
            at = base + i * slots + j
            left = jnp.concatenate([gains_ref[i, j], gains_ref[i, j + 1]], axis=1)
            right = jnp.concatenate([held[ids[at]], held[ids[at + 1]]], axis=0)
            part = jnp.dot(left, right, preferred_element_type=F32)
            acc = part if acc is None else acc + part
        out_ref[i] = acc


def pixel_pass(ids, meta, gains, other, sources, spans, rows, blocks, width):
    tiles, slots, block, _ = gains.shape
    tiles //= 2
    per_step = math.gcd(tiles, 8)
    steps = tiles // per_step
    count = len(sources)
    return pl.pallas_call(
        functools.partial(
            pixel_kernel,
            other=other,
            spans=spans,
            rows=rows,
            slots=slots,
            per_step=per_step,
            steps=steps,
        ),
        out_shape=jax.ShapeDtypeStruct((tiles, block, width), F32),
        grid_spec=pltpu.PrefetchScalarGridSpec(
            num_scalar_prefetch=2,
            grid=(steps,),
            in_specs=[
                pl.BlockSpec(
                    (per_step, slots, block, block),
                    lambda i, s, m: (half_start(m, other) * steps + i, 0, 0, 0),
                )
            ]
            + [pl.BlockSpec(memory_space=pl.ANY)] * count,
            out_specs=pl.BlockSpec((per_step, block, width), lambda i, s, m: (i, 0, 0)),
            scratch_shapes=[
                pltpu.VMEM((blocks, block, width), BF16),
                pltpu.SemaphoreType.DMA((count,)),
            ],
        ),
        cost_estimate=cost(
            2 * tiles * slots * block * block * width,
            2 * tiles * slots * block * block + 2 * blocks * block * width,
        ),
        name="pixel_pass",
    )(ids, meta, gains, *sources)


def whole(shape):
    return pl.BlockSpec(shape, lambda *_: (0,) * len(shape))


def share_kernel(mine, theirs, total, coded, *, groups):
    v = mine[...] + theirs[...]
    total[...] = v
    tiles, block, width = v.shape
    encode(v.reshape(tiles * block // SUB, SUB, width), coded, groups)


def share(mine, theirs, g):
    tiles, block, width = mine.shape
    tiles //= GROUPS
    n = tiles * block // SUB
    groups = math.gcd(tiles, SUB)
    size = tiles * block * width
    part = pl.BlockSpec((tiles, block, width), lambda i: (g, 0, 0))
    return pl.pallas_call(
        functools.partial(share_kernel, groups=groups),
        out_shape=(
            jax.ShapeDtypeStruct((tiles, block, width), F32),
            jax.ShapeDtypeStruct((n + 1, SUB, width), S16),
        ),
        grid=(1,),
        in_specs=[part, part],
        out_specs=(whole((tiles, block, width)), whole((n + 1, SUB, width))),
        cost_estimate=cost(size * 8, size * 14),
        name="share",
    )(mine, theirs)


def finish_kernel(total, coded, out, *, groups):
    tiles, block, width = total.shape
    v = total[...] + decode(coded, groups).reshape(tiles, block, width)
    out[...] = v.astype(BF16)


def finish(total, coded):
    groups = math.gcd(total.shape[0], SUB)
    return pl.pallas_call(
        functools.partial(finish_kernel, groups=groups),
        out_shape=jax.ShapeDtypeStruct(total.shape, BF16),
        cost_estimate=cost(total.size * 4, total.size * 8),
        name="finish",
    )(total, coded)


def beam_kernel(ids, meta, gains_ref, *refs, slots, per_step, half, runs):
    step = pl.program_id(0)
    out_ref = refs[-1]

    @pl.when(step == 0)
    def _():
        out_ref[...] = jnp.zeros_like(out_ref)

    base = tile_block(step, meta, half) * per_step * slots
    for i in range(per_step):
        rows = refs[0][i]
        for q in range(1, len(refs) - 1):
            rows = jnp.where(step >= q * runs, refs[q][i], rows)
        for j in range(slots):
            part = lax.dot_general(
                gains_ref[i, j], rows, (((0,), (0,)), ((), ())), preferred_element_type=F32
            )
            out_ref[ids[base + i * slots + j]] += part


def tile_block(step, meta, half):
    return jnp.where(step < half, meta[0] * half + step, (1 - meta[0]) * half + step - half)


def beam_pass(ids, meta, gains, groups, blocks):
    _, slots, block, _ = gains.shape
    tiles, _, width = groups[0].shape
    per_step = math.gcd(tiles, 8)
    runs = tiles // per_step
    half = runs * len(groups) // 2
    every = tiles * len(groups)

    def group_spec(q):
        return pl.BlockSpec(
            (per_step, block, width), lambda i, s, m: (jnp.clip(i - q * runs, 0, runs - 1), 0, 0)
        )

    return pl.pallas_call(
        functools.partial(beam_kernel, slots=slots, per_step=per_step, half=half, runs=runs),
        out_shape=jax.ShapeDtypeStruct((blocks, block, width), F32),
        grid_spec=pltpu.PrefetchScalarGridSpec(
            num_scalar_prefetch=2,
            grid=(2 * half,),
            in_specs=[
                pl.BlockSpec(
                    (per_step, slots, block, block),
                    lambda i, s, m: (tile_block(i, m, half), 0, 0, 0),
                ),
            ]
            + [group_spec(q) for q in range(len(groups))],
            out_specs=pl.BlockSpec((blocks, block, width), lambda i, s, m: (0, 0, 0)),
        ),
        cost_estimate=cost(
            2 * every * slots * block * block * width,
            2 * every * slots * block * block + 4 * blocks * block * width,
        ),
        name="beam_pass",
    )(ids, meta, gains, *groups)


def own_specs(count, tiles, width, piece, where):
    if count == 3:
        return pl.BlockSpec((tiles, SUB, width), lambda i, m: (piece, m[1 + where], 0))
    return pl.BlockSpec((None, tiles, SUB, width), lambda i, m: (m[1 + where], piece, 0, 0))


def hop_kernel(meta, *refs, sums, arrivals, groups, final):
    refs = list(refs)
    for a in range(len(arrivals)):
        own = [refs.pop(0)[...] for _ in range(sums)]
        v = functools.reduce(lambda p, q: p + q, own)
        for _ in range(arrivals[a]):
            v = v + decode(refs.pop(0), groups)
        out = refs[-len(arrivals) + a] if not final else refs[0]
        if final:
            out[...] = v
        else:
            encode(v, out, groups)


def hop(meta, partials, places, piece, tiles, arrivals):
    width = partials[0].shape[-1]
    groups = math.gcd(tiles, SUB)
    operands, specs = [], []
    for a, message in enumerate(arrivals):
        for p in partials:
            operands.append(p)
            specs.append(own_specs(p.ndim, tiles, width, piece, places[a]))
        if message is not None:
            operands.append(message)
            specs.append(whole(message.shape))
    shape = jax.ShapeDtypeStruct((tiles + 1, SUB, width), S16)
    size = tiles * SUB * width
    return pl.pallas_call(
        functools.partial(
            hop_kernel,
            sums=len(partials),
            arrivals=[int(m is not None) for m in arrivals],
            groups=groups,
            final=False,
        ),
        out_shape=[shape] * len(arrivals),
        grid_spec=pltpu.PrefetchScalarGridSpec(
            num_scalar_prefetch=1,
            grid=(1,),
            in_specs=specs,
            out_specs=[whole(shape.shape)] * len(arrivals),
        ),
        cost_estimate=cost(size * 12, size * 14),
        name="hop",
    )(meta, *operands)


def last_kernel(meta, *refs, sums, count, groups, earlier):
    v = functools.reduce(lambda p, q: p + q, [r[...] for r in refs[:sums]])
    for m in refs[sums : sums + count]:
        v = v + decode(m, groups)
    flat = v.reshape(-1, v.shape[-1])
    out, gram = refs[-2:]
    out[...] = flat
    contract = (((0,), (0,)), ((), ()))
    if earlier:
        before = refs[sums + count][...]
        gram[0] = lax.dot_general(before, flat, contract, precision=HIGHEST, preferred_element_type=F32)
    gram[gram.shape[0] - 1] = lax.dot_general(flat, flat, contract, precision=HIGHEST, preferred_element_type=F32)


def last(meta, partials, piece, tiles, arrivals, before):
    width = partials[0].shape[-1]
    groups = math.gcd(tiles, SUB)
    operands = list(partials) + list(arrivals)
    specs = [own_specs(p.ndim, tiles, width, piece, 0) for p in partials]
    specs += [whole(m.shape) for m in arrivals]
    if before is not None:
        operands.append(before)
        specs.append(whole(before.shape))
    rows = tiles * SUB
    grams = 1 if before is None else 2
    return pl.pallas_call(
        functools.partial(
            last_kernel,
            sums=len(partials),
            count=len(arrivals),
            groups=groups,
            earlier=before is not None,
        ),
        out_shape=(
            jax.ShapeDtypeStruct((rows, width), F32),
            jax.ShapeDtypeStruct((grams, width, width), F32),
        ),
        grid_spec=pltpu.PrefetchScalarGridSpec(
            num_scalar_prefetch=1,
            grid=(1,),
            in_specs=specs,
            out_specs=[whole((rows, width)), whole((grams, width, width))],
        ),
        cost_estimate=cost(12 * grams * rows * width * width, rows * width * 20),
        name="last",
    )(meta, *operands)


def product(a, b):
    return jnp.dot(a, b, precision=HIGHEST, preferred_element_type=F32)


def inverse_of(lower):
    n = lower.shape[0]
    row = lax.broadcasted_iota(jnp.int32, (n, n), 0)
    column = lax.broadcasted_iota(jnp.int32, (n, n), 1)
    unit = jnp.where(row == column, 1.0, 0.0).astype(F32)
    lower = jnp.where(row >= column, lower, 0.0)
    diagonal = jnp.sum(lower * unit, axis=1, keepdims=True)
    scaled = lower / diagonal
    size = 8
    off = jnp.where(row // size == column // size, unit - scaled, 0.0)
    inverse = unit + off
    power = off
    for _ in range(2):
        power = product(power, power)
        inverse = inverse + product(inverse, power)
    while size < n:
        pair = (row // (2 * size) == column // (2 * size)) & (row // size != column // size)
        cross = jnp.where(pair, scaled, 0.0)
        inverse = inverse - product(product(inverse, cross), inverse)
        size *= 2
    across = jnp.sum(unit * (1.0 / diagonal), axis=0, keepdims=True)
    return inverse * across


def apply_kernel(*refs, count):
    lower, out, inverse = refs[count:]
    rows = refs[0].shape[0]
    inverse[...] = inverse_of(lower[...])
    right = inverse[...].T
    for p in range(count):
        out[pl.ds(p * rows, rows), :] = product(refs[p][...], right)


def apply_first(pieces, lower):
    rows, width = pieces[0].shape
    n = len(pieces)
    return pl.pallas_call(
        functools.partial(apply_kernel, count=n),
        out_shape=(
            jax.ShapeDtypeStruct((rows * n, width), F32),
            jax.ShapeDtypeStruct((width, width), F32),
        ),
        cost_estimate=cost(12 * n * rows * width * width, 8 * n * rows * width),
        name="apply_first",
    )(*pieces, lower)


def basis_kernel(*refs, count, scale):
    first, cross, lower, out = refs[count:]
    rows, width = refs[0].shape
    right = inverse_of(lower[...]).T
    for p in range(count):
        at = pl.ds(p * rows, rows)
        q = first[at, :]
        v = product(refs[p][...] - product(q, cross[...]), right)
        out[at, 0:width] = q * scale
        out[at, width : 2 * width] = v * scale


def apply_both(pieces, first, cross, lower, scale):
    rows, width = pieces[0].shape
    n = len(pieces)
    return pl.pallas_call(
        functools.partial(basis_kernel, count=n, scale=scale),
        out_shape=jax.ShapeDtypeStruct((rows * n, 2 * width), F32),
        cost_estimate=cost(24 * n * rows * width * width, 16 * n * rows * width),
        name="apply_both",
    )(*pieces, first, cross, lower)


def plan_of(n_pix):
    far, near = n_pix // 2, n_pix - 1 - n_pix // 2
    pieces, groups = range(PIECES), range(GROUPS)
    gather = [[("ag", c, h, s) for s in pieces for _ in (0,)] for c in (0, 1) for h in range(far)]
    first, second = gather[:far], gather[far:]
    fill = [
        [("k1t", 0)],
        [("k1m", 0)],
        [item for g in groups for item in (("share", 0, g), ("y", 0, g))],
    ]
    plan = [item for step in first for item in step]
    for h, step in enumerate(second):
        plan += step
        if h < len(fill):
            plan += fill[h]
    for rest in fill[len(second) :]:
        plan += rest
    plan += [("k1t", 1), ("fin", 0, 0), ("core", 0, 0), ("k1m", 1)]
    for g in range(1, GROUPS):
        plan += [("fin", 0, g), ("core", 0, g)]
    plan += [item for g in groups for item in (("share", 1, g), ("y", 1, g))]
    plan += [("k4", 0)]

    def ring(c, h):
        return [item for s in pieces for item in (("hop", c, h, s), ("rs", c, h, s))]

    for h in range(far):
        plan += ring(0, h)
        if h == far // 2:
            plan += [item for g in groups for item in (("fin", 1, g), ("core", 1, g))]
        if h == far - 1:
            plan += [("k4", 1)]
    plan += [("last", 0, s) for s in pieces]
    plan += ring(1, 0)
    for h in range(1, far):
        plan += ring(1, h)
        if h == far - 2:
            plan += [("first",)]
    plan += [("last", 1, s) for s in pieces]
    return plan, (far, near)


def solution(mesh):
    n_pix, n_beam = mesh.shape["pix"], mesh.shape["beam"]
    cycle = list(range(0, n_pix, 2)) + list(range(1, n_pix, 2))[::-1]
    onward = [(cycle[i], cycle[(i + 1) % n_pix]) for i in range(n_pix)]
    backward = [(b, a) for a, b in onward]
    inner = [(b, b ^ 1) for b in range(n_beam)]
    outer = [(b, b ^ 2) for b in range(n_beam)]
    table = np.zeros((n_pix * n_beam, 1 + n_pix), np.int32)
    for p in range(n_pix):
        around = [cycle[(cycle.index(p) + r) % n_pix] for r in range(n_pix)]
        for b in range(n_beam):
            table[p * n_beam + b] = [b % 2] + around
    plan, near_far = plan_of(n_pix)
    hops = [near_far, near_far[::-1]]
    most = max(near_far)

    def local(sketch, gains, coverage):
        blocks, rows, columns = sketch.shape
        block = gains.shape[2]
        beams = blocks * n_beam * block
        width = columns // 2
        aligned = rows == SUB
        ids = coverage.reshape(-1)
        device = lax.axis_index("pix") * n_beam + lax.axis_index("beam")
        meta = lax.dynamic_index_in_dim(jnp.asarray(table), device, keepdims=False)
        per_piece = blocks // PIECES
        tiles_piece = per_piece * rows // SUB
        own = {
            (c, s): sketch[s * per_piece : (s + 1) * per_piece, :, c * width : (c + 1) * width]
            for c in (0, 1)
            for s in range(PIECES)
        }
        flow, held, got = {}, {}, {}

        def sources_of(c):
            sources, spans = [], []
            for s in range(PIECES):
                offsets = {0: own[c, s]}
                for (d, h), x in sorted(flow["ag", c, s].items()):
                    offsets[(n_pix - h - 1) if d == 0 else (h + 1)] = x
                if aligned:
                    for r in sorted(offsets):
                        sources.append(offsets[r])
                        spans.append((s * per_piece, per_piece, r))
                else:
                    stack = jnp.stack([offsets[r] for r in range(n_pix)])
                    stack = stack[jnp.argsort(meta[1:])]
                    stack = stack.transpose(1, 0, 2, 3).reshape(per_piece, block, width)
                    sources.append(stack)
                    spans.append((s * per_piece, per_piece, None))
            return sources, spans

        def sweep(c, other):
            if ("sources", c) not in got:
                got["sources", c] = sources_of(c)
            sources, spans = got["sources", c]
            return pixel_pass(
                ids, meta, gains, other, sources, spans, rows if aligned else block, blocks, width
            )

        def partials_of(x):
            if aligned:
                return x
            x = x.reshape(blocks, n_pix, rows, width).transpose(1, 0, 2, 3)
            return x.reshape(n_pix, blocks * rows // SUB, SUB, width)

        def everywhere(g):
            for axis, number in (("beam", n_beam), ("pix", n_pix)):
                stride = 1
                while stride < number:
                    g = g + lax.ppermute(g, axis, [(b, b ^ stride) for b in range(number)])
                    stride *= 2
            return g

        def run(item):
            kind, c = item[0], item[1] if len(item) > 1 else None
            if kind == "ag":
                _, _, h, s = item
                flows = flow.setdefault(("ag", c, s), {})
                for d, ring in enumerate((onward, backward)):
                    if h < hops[c][d]:
                        before = own[c, s] if h == 0 else flows[d, h - 1]
                        flows[d, h] = lax.ppermute(before, "pix", ring)
            elif kind == "k1t":
                held["away", c] = sweep(c, True)
                held["away", c] = lax.ppermute(held["away", c], "beam", inner)
            elif kind == "k1m":
                held["kept", c] = sweep(c, False)
            elif kind == "share":
                g = item[2]
                held["total", c, g], held["coded", c, g] = share(held["kept", c], held["away", c], g)
            elif kind == "y":
                g = item[2]
                held["came", c, g] = lax.ppermute(held["coded", c, g], "beam", outer)
            elif kind == "fin":
                g = item[2]
                held["zb", c, g] = finish(held["total", c, g], held["came", c, g])
            elif kind == "core":
                g = item[2]
                held["peer", c, g] = lax.ppermute(held["zb", c, g], "beam", inner)
            elif kind == "k4":
                groups = [held[k, c, g] for k in ("zb", "peer") for g in range(GROUPS)]
                held["sums", c] = partials_of(beam_pass(ids, meta, gains, groups, blocks))
            elif kind == "hop":
                _, _, h, s = item
                live = [d for d in (0, 1) if h >= most - hops[c][d]]
                left = most - h
                places = [left if d == 0 else n_pix - left for d in live]
                came = [None if h == most - hops[c][d] else flow["rs", c, s, d] for d in live]
                sent = hop(meta, [held["sums", c]], places, s, tiles_piece, came)
                for d, message in zip(live, sent):
                    held["sent", c, s, d] = message
            elif kind == "rs":
                _, _, h, s = item
                for d, ring in enumerate((onward, backward)):
                    if h >= most - hops[c][d]:
                        flow["rs", c, s, d] = lax.ppermute(held["sent", c, s, d], "pix", ring)
            elif kind == "last":
                s = item[2]
                came = [flow["rs", c, s, d] for d in (0, 1) if ("rs", c, s, d) in flow]
                before = held["y", 0, s] if c else None
                held["y", c, s], held["gram", c, s] = last(
                    meta, [held["sums", c]], s, tiles_piece, came, before
                )
            elif kind == "first":
                gram = sum(held["gram", 0, s] for s in range(PIECES))
                held["lower", 0] = jnp.linalg.cholesky(everywhere(gram)[0])
                pieces = [held["y", 0, s] for s in range(PIECES)]
                held["q"], held["inverse"] = apply_first(pieces, held["lower", 0])

        for item in plan:
            run(item)
        gram = everywhere(sum(held["gram", 1, s] for s in range(PIECES)))
        r12 = jnp.dot(held["inverse"], gram[0], precision=HIGHEST)
        rest = gram[1] - jnp.dot(r12.T, r12, precision=HIGHEST)
        lower = jnp.linalg.cholesky(rest)
        scale = math.sqrt(float(beams))
        pieces = [held["y", 1, s] for s in range(PIECES)]
        basis = apply_both(pieces, held["q"], r12, lower, scale)
        top = jnp.concatenate([held["lower", 0].T, r12], axis=1)
        low = jnp.concatenate([jnp.zeros_like(r12), lower.T], axis=1)
        factor = jnp.concatenate([top, low], axis=0) / scale
        return basis.reshape(blocks, rows, columns), factor

    return jax.shard_map(
        local,
        mesh=mesh,
        in_specs=(P("beam", "pix", None), P("pix", "beam", None, None), P("pix", "beam")),
        out_specs=(P("beam", "pix", None), P()),
        check_vma=False,
    )
```

```python
import functools
import math

import jax
import jax.numpy as jnp
import numpy as np
from jax import lax
from jax.experimental import pallas as pl
from jax.experimental.pallas import tpu as pltpu
from jax.sharding import PartitionSpec as P

BF16, F32, S16 = jnp.bfloat16, jnp.float32, jnp.int16
HIGHEST = lax.Precision.HIGHEST
SUB = 16
STEPS = 256.0
TOP = 32760.0
LEAST = 1e-30
PART = 64
GATHER_PIECES = (2, 2)
SCATTER_PIECES = (1, 2)
ROOM = pltpu.CompilerParams(vmem_limit_bytes=67043328)


def cost(flops, nbytes):
    return pl.CostEstimate(flops=int(flops), bytes_accessed=int(nbytes), transcendentals=0)


def encode(v, out, groups):
    n, sub, width = v.shape
    g = v.reshape(groups, n // groups * sub, width)
    peak = jnp.maximum(jnp.max(jnp.abs(g), axis=1), LEAST)
    power = jnp.ceil(jnp.log2(peak) * STEPS)
    gain = jnp.exp2(power * (-1.0 / STEPS)) * TOP
    q = jnp.round(g * gain[:, None, :]).reshape(n, sub, width)
    out[0:n] = q.astype(jnp.int32).astype(S16)
    if groups < sub:
        power = jnp.concatenate([power, jnp.zeros((sub - groups, width), F32)], axis=0)
    out[n] = power.astype(jnp.int32).astype(S16)


def decode(msg, groups):
    n = msg.shape[0] - 1
    sub, width = msg.shape[1:]
    power = msg[n].astype(jnp.int32).astype(F32)[0:groups]
    gain = jnp.exp2(power * (1.0 / STEPS)) * (1.0 / TOP)
    q = msg[0:n].astype(jnp.int32).astype(F32).reshape(groups, n // groups * sub, width)
    return (q * gain[:, None, :]).reshape(n, sub, width)


UNROLL = 4


def half_tiles(step, meta, half):
    return jnp.where(step < half, (1 - meta[0]) * half + step, meta[0] * half + step - half)


def pixel_kernel(ids, meta, *refs, spans, rows, slots, per_step, half):
    count = len(spans)
    gains_ref, sources = refs[0], refs[1 : 1 + count]
    away_ref, kept_ref, held, sems = refs[1 + count :]
    step = pl.program_id(0)

    @pl.when(step == 0)
    def _():
        copies = []
        for m in range(count):
            first, number, offset = spans[m]
            start = 0 if offset is None else pl.multiple_of(meta[1 + offset] * rows, rows)
            target = held.at[pl.ds(first, number), pl.ds(start, rows), :]
            copies.append(pltpu.make_async_copy(sources[m], target, sems.at[m]))
        for c in copies:
            c.start()
        for c in copies:
            c.wait()

    base = half_tiles(step, meta, half) * per_step * slots

    def sweep(out_ref):
        def some(k, _):
            for r in range(UNROLL):
                i = k * UNROLL + r
                acc = None
                for j in range(0, slots, 2):
                    at = base + i * slots + j
                    left = jnp.concatenate([gains_ref[i, j], gains_ref[i, j + 1]], axis=1)
                    right = jnp.concatenate([held[ids[at]], held[ids[at + 1]]], axis=0)
                    part = jnp.dot(left, right, preferred_element_type=F32)
                    acc = part if acc is None else acc + part
                out_ref[i] = acc
            return 0

        lax.fori_loop(0, per_step // UNROLL, some, 0)

    pl.when(step < half)(lambda: sweep(away_ref))
    pl.when(step >= half)(lambda: sweep(kept_ref))


def pixel_pass(ids, meta, gains, sources, spans, rows, blocks, width):
    tiles, slots, block, _ = gains.shape
    tiles //= 2
    per_step = math.gcd(tiles, 16)
    half = tiles // per_step
    count = len(sources)
    out = jax.ShapeDtypeStruct((tiles, block, width), F32)
    return pl.pallas_call(
        functools.partial(
            pixel_kernel, spans=spans, rows=rows, slots=slots, per_step=per_step, half=half
        ),
        out_shape=(out, out),
        grid_spec=pltpu.PrefetchScalarGridSpec(
            num_scalar_prefetch=2,
            grid=(2 * half,),
            in_specs=[
                pl.BlockSpec(
                    (per_step, slots, block, block),
                    lambda i, s, m: (half_tiles(i, m, half), 0, 0, 0),
                )
            ]
            + [pl.BlockSpec(memory_space=pl.ANY)] * count,
            out_specs=(
                pl.BlockSpec(
                    (per_step, block, width), lambda i, s, m: (jnp.minimum(i, half - 1), 0, 0)
                ),
                pl.BlockSpec(
                    (per_step, block, width), lambda i, s, m: (jnp.maximum(i - half, 0), 0, 0)
                ),
            ),
            scratch_shapes=[
                pltpu.VMEM((blocks, block, width), BF16),
                pltpu.SemaphoreType.DMA((count,)),
            ],
        ),
        cost_estimate=cost(
            4 * tiles * slots * block * block * width,
            4 * tiles * slots * block * block + 2 * blocks * block * width,
        ),
        name="pixel_pass",
    )(ids, meta, gains, *sources)


def whole(shape):
    return pl.BlockSpec(shape, lambda *_: (0,) * len(shape))


def share_kernel(mine, theirs, total, coded, *, groups):
    v = mine[...] + theirs[...]
    total[...] = v
    tiles, block, width = v.shape
    encode(v.reshape(tiles * block // SUB, SUB, width), coded, groups)


def share(mine, theirs):
    tiles, block, width = mine.shape
    per = PART * SUB * 2 // block
    parts, n = tiles // per, per * block // SUB
    part = pl.BlockSpec((per, block, width), lambda i: (i, 0, 0))
    return pl.pallas_call(
        functools.partial(share_kernel, groups=SUB),
        out_shape=(
            jax.ShapeDtypeStruct(mine.shape, F32),
            jax.ShapeDtypeStruct((parts * (n + 1), SUB, width), S16),
        ),
        grid=(parts,),
        in_specs=[part, part],
        out_specs=(part, pl.BlockSpec((n + 1, SUB, width), lambda i: (i, 0, 0))),
        cost_estimate=cost(mine.size * 8, mine.size * 14),
        compiler_params=ROOM,
        name="share",
    )(mine, theirs)


def finish_kernel(total, coded, out, *, groups):
    tiles, block, width = total.shape
    v = total[...] + decode(coded, groups).reshape(tiles, block, width)
    out[...] = v.astype(BF16)


def finish(total, coded):
    tiles, block, width = total.shape
    per = PART * SUB * 2 // block
    parts, n = tiles // per, per * block // SUB
    part = pl.BlockSpec((per, block, width), lambda i: (i, 0, 0))
    return pl.pallas_call(
        functools.partial(finish_kernel, groups=SUB),
        out_shape=jax.ShapeDtypeStruct(total.shape, BF16),
        grid=(parts,),
        in_specs=[part, pl.BlockSpec((n + 1, SUB, width), lambda i: (i, 0, 0))],
        out_specs=part,
        cost_estimate=cost(total.size * 4, total.size * 8),
        compiler_params=ROOM,
        name="finish",
    )(total, coded)


def beam_kernel(ids, meta, gains_ref, theirs, mine, out_ref, *, slots, per_step, half):
    step = pl.program_id(0)

    @pl.when(step == 0)
    def _():
        out_ref[...] = jnp.zeros_like(out_ref)

    base = half_tiles(step, meta, half) * per_step * slots

    def sweep(source):
        def some(k, _):
            for r in range(UNROLL):
                i = k * UNROLL + r
                rows = source[i]
                for j in range(slots):
                    part = lax.dot_general(
                        gains_ref[i, j], rows, (((0,), (0,)), ((), ())), preferred_element_type=F32
                    )
                    out_ref[ids[base + i * slots + j]] += part
            return 0

        lax.fori_loop(0, per_step // UNROLL, some, 0)

    pl.when(step < half)(lambda: sweep(theirs))
    pl.when(step >= half)(lambda: sweep(mine))


def beam_pass(ids, meta, gains, theirs, mine, blocks):
    _, slots, block, _ = gains.shape
    tiles, _, width = mine.shape
    per_step = math.gcd(tiles, 16)
    half = tiles // per_step
    return pl.pallas_call(
        functools.partial(beam_kernel, slots=slots, per_step=per_step, half=half),
        out_shape=jax.ShapeDtypeStruct((blocks, block, width), F32),
        grid_spec=pltpu.PrefetchScalarGridSpec(
            num_scalar_prefetch=2,
            grid=(2 * half,),
            in_specs=[
                pl.BlockSpec(
                    (per_step, slots, block, block),
                    lambda i, s, m: (half_tiles(i, m, half), 0, 0, 0),
                ),
                pl.BlockSpec(
                    (per_step, block, width), lambda i, s, m: (jnp.minimum(i, half - 1), 0, 0)
                ),
                pl.BlockSpec(
                    (per_step, block, width), lambda i, s, m: (jnp.maximum(i - half, 0), 0, 0)
                ),
            ],
            out_specs=pl.BlockSpec((blocks, block, width), lambda i, s, m: (0, 0, 0)),
        ),
        cost_estimate=cost(
            4 * tiles * slots * block * block * width,
            4 * tiles * slots * block * block + 4 * blocks * block * width,
        ),
        name="beam_pass",
    )(ids, meta, gains, theirs, mine)


def own_spec(sums, part, first, where):
    width = sums.shape[-1]
    if sums.ndim == 3:
        return pl.BlockSpec((part, SUB, width), lambda i, m: (first + i, m[1 + where], 0))
    return pl.BlockSpec((None, part, SUB, width), lambda i, m: (m[1 + where], first + i, 0, 0))


def part_spec(rows, width):
    return pl.BlockSpec((rows, SUB, width), lambda i, m: (i, 0, 0))


def hop_kernel(meta, *refs, arrivals, groups):
    ins, outs = list(refs[: -len(arrivals)]), refs[-len(arrivals) :]
    for came, out in zip(arrivals, outs):
        v = ins.pop(0)[...]
        if came:
            v = v + decode(ins.pop(0), groups)
        encode(v, out, groups)


def hop(meta, sums, places, first, tiles, arrivals):
    width = sums.shape[-1]
    part = math.gcd(tiles, PART)
    parts = tiles // part
    operands, specs = [], []
    for where, message in zip(places, arrivals):
        operands.append(sums)
        specs.append(own_spec(sums, part, first // part, where))
        if message is not None:
            operands.append(message)
            specs.append(part_spec(part + 1, width))
    shape = jax.ShapeDtypeStruct((parts * (part + 1), SUB, width), S16)
    size = tiles * SUB * width * len(arrivals)
    return pl.pallas_call(
        functools.partial(
            hop_kernel,
            arrivals=[m is not None for m in arrivals],
            groups=math.gcd(part, SUB),
        ),
        out_shape=[shape] * len(arrivals),
        grid_spec=pltpu.PrefetchScalarGridSpec(
            num_scalar_prefetch=1,
            grid=(parts,),
            in_specs=specs,
            out_specs=[part_spec(part + 1, width)] * len(arrivals),
        ),
        cost_estimate=cost(size * 6, size * 8),
        compiler_params=ROOM,
        name="hop",
    )(meta, *operands)


def add(a, b):
    def kernel(a_ref, b_ref, out_ref):
        out_ref[...] = a_ref[...] + b_ref[...]

    return pl.pallas_call(
        kernel, out_shape=jax.ShapeDtypeStruct(a.shape, a.dtype), compiler_params=ROOM, name="add"
    )(a, b)


def last_kernel(meta, *refs, count, groups, earlier, chained):
    v = refs[0][...]
    for m in refs[1 : 1 + count]:
        v = v + decode(m, groups)
    flat = v.reshape(-1, v.shape[-1])
    out, gram = refs[-2:]
    out[...] = flat

    @pl.when(pl.program_id(0) == 0)
    def _():
        gram[...] = refs[-3][...] if chained else jnp.zeros_like(gram)

    def inner_products(a, b):
        return lax.dot_general(
            a, b, (((0,), (0,)), ((), ())), precision=HIGHEST, preferred_element_type=F32
        )

    if earlier:
        gram[0] += inner_products(refs[1 + count][...], flat)
    gram[gram.shape[0] - 1] += inner_products(flat, flat)


def last(meta, sums, first, tiles, arrivals, before, gram):
    width = sums.shape[-1]
    part = math.gcd(tiles, PART)
    parts, rows = tiles // part, part * SUB
    operands = [sums, *arrivals]
    specs = [own_spec(sums, part, first // part, 0)]
    specs += [part_spec(part + 1, width)] * len(arrivals)
    if before is not None:
        operands.append(before)
        specs.append(pl.BlockSpec((rows, width), lambda i, m: (first // part + i, 0)))
    grams = 1 if before is None else 2
    if gram is not None:
        operands.append(gram)
        specs.append(whole(gram.shape))
    return pl.pallas_call(
        functools.partial(
            last_kernel,
            count=len(arrivals),
            groups=math.gcd(part, SUB),
            earlier=before is not None,
            chained=gram is not None,
        ),
        out_shape=(
            jax.ShapeDtypeStruct((tiles * SUB, width), F32),
            jax.ShapeDtypeStruct((grams, width, width), F32),
        ),
        grid_spec=pltpu.PrefetchScalarGridSpec(
            num_scalar_prefetch=1,
            grid=(parts,),
            in_specs=specs,
            out_specs=[pl.BlockSpec((rows, width), lambda i, m: (i, 0)), whole((grams, width, width))],
        ),
        cost_estimate=cost(12 * grams * tiles * SUB * width * width, tiles * SUB * width * 12),
        compiler_params=ROOM,
        name="last",
    )(meta, *operands)


def product(a, b):
    return jnp.dot(a, b, precision=HIGHEST, preferred_element_type=F32)


def inverse_of(lower):
    n = lower.shape[0]
    row = lax.broadcasted_iota(jnp.int32, (n, n), 0)
    column = lax.broadcasted_iota(jnp.int32, (n, n), 1)
    unit = jnp.where(row == column, 1.0, 0.0).astype(F32)
    lower = jnp.where(row >= column, lower, 0.0)
    diagonal = jnp.sum(lower * unit, axis=1, keepdims=True)
    scaled = lower / diagonal
    size = 8
    off = jnp.where(row // size == column // size, unit - scaled, 0.0)
    inverse = unit + off
    power = off
    for _ in range(2):
        power = product(power, power)
        inverse = inverse + product(inverse, power)
    while size < n:
        pair = (row // (2 * size) == column // (2 * size)) & (row // size != column // size)
        cross = jnp.where(pair, scaled, 0.0)
        inverse = inverse - product(product(inverse, cross), inverse)
        size *= 2
    across = jnp.sum(unit * (1.0 / diagonal), axis=0, keepdims=True)
    return inverse * across


def apply_kernel(*refs, count):
    lower, out, inverse = refs[count:]
    rows = refs[0].shape[0]
    inverse[...] = inverse_of(lower[...])
    right = inverse[...].T
    for p in range(count):
        out[pl.ds(p * rows, rows), :] = product(refs[p][...], right)


def apply_first(pieces, lower):
    rows, width = pieces[0].shape
    n = len(pieces)
    return pl.pallas_call(
        functools.partial(apply_kernel, count=n),
        out_shape=(
            jax.ShapeDtypeStruct((rows * n, width), F32),
            jax.ShapeDtypeStruct((width, width), F32),
        ),
        cost_estimate=cost(12 * n * rows * width * width, 8 * n * rows * width),
        name="apply_first",
    )(*pieces, lower)


def basis_kernel(*refs, count, scale):
    first, cross, lower, out = refs[count:]
    rows, width = refs[0].shape
    right = inverse_of(lower[...]).T
    for p in range(count):
        at = pl.ds(p * rows, rows)
        q = first[at, :]
        v = product(refs[p][...] - product(q, cross[...]), right)
        out[at, 0:width] = q * scale
        out[at, width : 2 * width] = v * scale


def apply_both(pieces, first, cross, lower, scale):
    rows, width = pieces[0].shape
    n = len(pieces)
    return pl.pallas_call(
        functools.partial(basis_kernel, count=n, scale=scale),
        out_shape=jax.ShapeDtypeStruct((rows * n, 2 * width), F32),
        cost_estimate=cost(24 * n * rows * width * width, 16 * n * rows * width),
        name="apply_both",
    )(*pieces, first, cross, lower)


def plan_of(far):
    def gather(c, h):
        return [("ag", c, h, s) for s in range(GATHER_PIECES[c])]

    def scatter(c, h, s):
        return [("hop", c, h, s), ("rs", c, h, s)]

    plan = [item for h in range(far) for item in gather(0, h)] + gather(1, 0)
    plan += [("k1", 0), ("swap", 0)] + gather(1, 1) + [("share", 0), ("y", 0)]
    for h in range(2, far):
        plan += gather(1, h)
    plan += [("fin", 0), ("core", 0), ("k4", 0)]

    def first(h):
        return [item for s in range(SCATTER_PIECES[0]) for item in scatter(0, h, s)]

    plan += first(0) + [("k1", 1), ("swap", 1)] + first(1) + [("share", 1), ("y", 1)]
    for h in range(2, far):
        plan += first(h)
    plan += [("fin", 1), ("core", 1), ("k4", 1)]
    steps = [(h, s) for h in range(far) for s in range(SCATTER_PIECES[1])]
    for k, (h, s) in enumerate(steps):
        plan += scatter(1, h, s)
        if k == 0:
            plan += [("last", 0, p) for p in range(SCATTER_PIECES[0])]
        plan += [("add", 0, k - 1)] if k else []
        plan += [("ar", 0, k)]
    plan += [("last", 1, s) for s in range(SCATTER_PIECES[1])]
    plan += [("ar", 1, 0), ("ar", 1, 1), ("chol", 0), ("ar", 1, 2), ("first", 0), ("ar", 1, 3)]
    return plan


def solution(mesh):
    n_pix, n_beam = mesh.shape["pix"], mesh.shape["beam"]
    cycle = list(range(0, n_pix, 2)) + list(range(1, n_pix, 2))[::-1]
    onward = [(cycle[i], cycle[(i + 1) % n_pix]) for i in range(n_pix)]
    backward = [(b, a) for a, b in onward]
    inner = [(b, b ^ 1) for b in range(n_beam)]
    outer = [(b, b ^ 2) for b in range(n_beam)]
    table = np.zeros((n_pix * n_beam, 1 + n_pix), np.int32)
    for p in range(n_pix):
        around = [cycle[(cycle.index(p) + r) % n_pix] for r in range(n_pix)]
        for b in range(n_beam):
            table[p * n_beam + b] = [b % 2] + around
    most = n_pix // 2
    hops = [(most, n_pix - 1 - most), (n_pix - 1 - most, most)]
    strides = [(a, 2**k) for a, n in (("beam", n_beam), ("pix", n_pix)) for k in range(n.bit_length() - 1)]
    plan = plan_of(most)

    def local(sketch, gains, coverage):
        blocks, rows, columns = sketch.shape
        block = gains.shape[2]
        beams = blocks * n_beam * block
        width = columns // 2
        aligned = rows == SUB
        ids = coverage.reshape(-1)
        device = lax.axis_index("pix") * n_beam + lax.axis_index("beam")
        meta = lax.dynamic_index_in_dim(jnp.asarray(table), device, keepdims=False)
        tiles_here = blocks * rows // SUB
        own = {}
        for c in (0, 1):
            number = blocks // GATHER_PIECES[c]
            for p in range(GATHER_PIECES[c]):
                own[c, p] = sketch[p * number : (p + 1) * number, :, c * width : (c + 1) * width]
        flow, held = {}, {}

        def sources_of(c):
            sources, spans = [], []
            per_piece = blocks // GATHER_PIECES[c]
            for s in range(GATHER_PIECES[c]):
                offsets = {0: own[c, s]}
                for (d, h), x in sorted(flow["ag", c, s].items()):
                    offsets[(n_pix - h - 1) if d == 0 else (h + 1)] = x
                if aligned:
                    for r in sorted(offsets):
                        sources.append(offsets[r])
                        spans.append((s * per_piece, per_piece, r))
                else:
                    stack = jnp.stack([offsets[r] for r in range(n_pix)])
                    stack = stack[jnp.argsort(meta[1:])]
                    stack = stack.transpose(1, 0, 2, 3).reshape(per_piece, block, width)
                    sources.append(stack)
                    spans.append((s * per_piece, per_piece, None))
            return sources, spans

        def partials_of(x):
            if aligned:
                return x
            x = x.reshape(blocks, n_pix, rows, width).transpose(1, 0, 2, 3)
            return x.reshape(n_pix, blocks * rows // SUB, SUB, width)

        def passed(g, k):
            axis, stride = strides[k]
            return lax.ppermute(g, axis, [(b, b ^ stride) for b in range(mesh.shape[axis])])

        def run(item):
            kind, c = item[0], item[1] if len(item) > 1 else None
            if kind == "ag":
                _, _, h, s = item
                flows = flow.setdefault(("ag", c, s), {})
                for d, ring in enumerate((onward, backward)):
                    if h < hops[c][d]:
                        before = own[c, s] if h == 0 else flows[d, h - 1]
                        flows[d, h] = lax.ppermute(before, "pix", ring)
            elif kind == "k1":
                sources, spans = sources_of(c)
                held["away", c], held["kept", c] = pixel_pass(
                    ids, meta, gains, sources, spans, rows if aligned else block, blocks, width
                )
            elif kind == "swap":
                held["away", c] = lax.ppermute(held["away", c], "beam", inner)
            elif kind == "share":
                held["total", c], held["coded", c] = share(held["kept", c], held["away", c])
            elif kind == "y":
                held["came", c] = lax.ppermute(held["coded", c], "beam", outer)
            elif kind == "fin":
                held["zb", c] = finish(held["total", c], held["came", c])
            elif kind == "core":
                held["peer", c] = lax.ppermute(held["zb", c], "beam", inner)
            elif kind == "k4":
                sums = beam_pass(ids, meta, gains, held["peer", c], held["zb", c], blocks)
                held["sums", c] = partials_of(sums)
            elif kind == "hop":
                _, _, h, s = item
                live = [d for d in (0, 1) if h >= most - hops[c][d]]
                left = most - h
                places = [left if d == 0 else n_pix - left for d in live]
                came = [None if h == most - hops[c][d] else flow["rs", c, s, d] for d in live]
                tiles = tiles_here // SCATTER_PIECES[c]
                sent = hop(meta, held["sums", c], places, s * tiles, tiles, came)
                for d, message in zip(live, sent):
                    held["sent", c, s, d] = message
            elif kind == "rs":
                _, _, h, s = item
                for d, ring in enumerate((onward, backward)):
                    if h >= most - hops[c][d]:
                        flow["rs", c, s, d] = lax.ppermute(held["sent", c, s, d], "pix", ring)
            elif kind == "last":
                s = item[2]
                came = [flow["rs", c, s, d] for d in (0, 1) if ("rs", c, s, d) in flow]
                tiles = tiles_here // SCATTER_PIECES[c]
                held["y", c, s], held["gram", c] = last(
                    meta,
                    held["sums", c],
                    s * tiles,
                    tiles,
                    came,
                    held["y", 0, 0] if c else None,
                    held.get(("gram", c)),
                )
            elif kind == "ar" and item[2] < len(strides):
                held["other", c] = passed(held["gram", c], item[2])
                if c:
                    held["gram", c] = held["gram", c] + held["other", c]
                held["stage", c] = item[2] + 1
            elif kind == "add" and item[2] < len(strides):
                held["gram", c] = add(held["gram", c], held["other", c])
                held["added", c] = item[2] + 1
            elif kind == "chol":
                g = held["gram", c]
                if held["added", c] < held["stage", c]:
                    g = g + held["other", c]
                for k in range(held["stage", c], len(strides)):
                    g = g + passed(g, k)
                held["lower"] = jnp.linalg.cholesky(g[0])
            elif kind == "first":
                held["q"], held["inverse"] = apply_first([held["y", 0, 0]], held["lower"])

        for item in plan:
            run(item)
        gram = held["gram", 1]
        for k in range(held["stage", 1], len(strides)):
            gram = gram + passed(gram, k)
        r12 = jnp.dot(held["inverse"], gram[0], precision=HIGHEST)
        rest = gram[1] - jnp.dot(r12.T, r12, precision=HIGHEST)
        lower = jnp.linalg.cholesky(rest)
        scale = math.sqrt(float(beams))
        pieces = [held["y", 1, s] for s in range(SCATTER_PIECES[1])]
        basis = apply_both(pieces, held["q"], r12, lower, scale)
        top = jnp.concatenate([held["lower"].T, r12], axis=1)
        low = jnp.concatenate([jnp.zeros_like(r12), lower.T], axis=1)
        factor = jnp.concatenate([top, low], axis=0) / scale
        return basis.reshape(blocks, rows, columns), factor

    return jax.shard_map(
        local,
        mesh=mesh,
        in_specs=(P("beam", "pix", None), P("pix", "beam", None, None), P("pix", "beam")),
        out_specs=(P("beam", "pix", None), P()),
        check_vma=False,
    )
```

```python
import functools
import math

import jax
import jax.numpy as jnp
import numpy as np
from jax import lax
from jax.experimental import pallas as pl
from jax.experimental.pallas import tpu as pltpu
from jax.sharding import PartitionSpec as P

BF16, F32, S16 = jnp.bfloat16, jnp.float32, jnp.int16
HIGHEST = lax.Precision.HIGHEST
SUB = 16
STEPS = 256.0
TOP = 32760.0
LEAST = 1e-30
PART = 64
GATHER_PIECES = (2, 2)
SCATTER_PIECES = (1, 1)
ROOM = pltpu.CompilerParams(vmem_limit_bytes=67043328)


def cost(flops, nbytes):
    return pl.CostEstimate(flops=int(flops), bytes_accessed=int(nbytes), transcendentals=0)


def encode(v, out, groups):
    n, sub, width = v.shape
    g = v.reshape(groups, n // groups * sub, width)
    peak = jnp.maximum(jnp.max(jnp.abs(g), axis=1), LEAST)
    power = jnp.ceil(jnp.log2(peak) * STEPS)
    gain = jnp.exp2(power * (-1.0 / STEPS)) * TOP
    q = jnp.round(g * gain[:, None, :]).reshape(n, sub, width)
    out[0:n] = q.astype(jnp.int32).astype(S16)
    if groups < sub:
        power = jnp.concatenate([power, jnp.zeros((sub - groups, width), F32)], axis=0)
    out[n] = power.astype(jnp.int32).astype(S16)


def decode(msg, groups):
    n = msg.shape[0] - 1
    sub, width = msg.shape[1:]
    power = msg[n].astype(jnp.int32).astype(F32)[0:groups]
    gain = jnp.exp2(power * (1.0 / STEPS)) * (1.0 / TOP)
    q = msg[0:n].astype(jnp.int32).astype(F32).reshape(groups, n // groups * sub, width)
    return (q * gain[:, None, :]).reshape(n, sub, width)


UNROLL = 16
STREAMS = 1


def gains_specs(per_step, slots, block, half):
    number = per_step // STREAMS
    return [
        pl.BlockSpec(
            (number, slots, block, block),
            lambda i, s, m, q=q: (half_tiles(i, m, half) * STREAMS + q, 0, 0, 0),
        )
        for q in range(STREAMS)
    ]


def half_tiles(step, meta, half):
    return jnp.where(step < half, (1 - meta[0]) * half + step, meta[0] * half + step - half)


def pixel_kernel(ids, meta, *refs, spans, rows, slots, per_step, half):
    count = len(spans)
    streams, sources = refs[:STREAMS], refs[STREAMS : STREAMS + count]
    away_ref, kept_ref, held, sems = refs[STREAMS + count :]
    step = pl.program_id(0)

    @pl.when(step == 0)
    def _():
        copies = []
        for m in range(count):
            first, number, offset = spans[m]
            start = 0 if offset is None else pl.multiple_of(meta[1 + offset] * rows, rows)
            target = held.at[pl.ds(first, number), pl.ds(start, rows), :]
            copies.append(pltpu.make_async_copy(sources[m], target, sems.at[m]))
        for c in copies:
            c.start()
        for c in copies:
            c.wait()

    base = half_tiles(step, meta, half) * per_step * slots

    def sweep(out_ref):
        for q in range(STREAMS):
            lax.fori_loop(
                0, streams[q].shape[0] // UNROLL, functools.partial(some, out_ref, q), 0
            )

    def some(out_ref, q, k, _):
            gains_ref = streams[q]
            for r in range(UNROLL):
                n = k * UNROLL + r
                i = q * gains_ref.shape[0] + n
                acc = None
                for j in range(0, slots, 2):
                    at = base + i * slots + j
                    left = jnp.concatenate([gains_ref[n, j], gains_ref[n, j + 1]], axis=1)
                    right = jnp.concatenate([held[ids[at]], held[ids[at + 1]]], axis=0)
                    part = jnp.dot(left, right, preferred_element_type=F32)
                    acc = part if acc is None else acc + part
                out_ref[i] = acc
            return 0

    pl.when(step < half)(lambda: sweep(away_ref))
    pl.when(step >= half)(lambda: sweep(kept_ref))


def pixel_pass(ids, meta, gains, sources, spans, rows, blocks, width):
    tiles, slots, block, _ = gains.shape
    tiles //= 2
    per_step = math.gcd(tiles, 16)
    half = tiles // per_step
    count = len(sources)
    out = jax.ShapeDtypeStruct((tiles, block, width), F32)
    return pl.pallas_call(
        functools.partial(
            pixel_kernel, spans=spans, rows=rows, slots=slots, per_step=per_step, half=half
        ),
        out_shape=(out, out),
        grid_spec=pltpu.PrefetchScalarGridSpec(
            num_scalar_prefetch=2,
            grid=(2 * half,),
            in_specs=gains_specs(per_step, slots, block, half)
            + [pl.BlockSpec(memory_space=pl.ANY)] * count,
            out_specs=(
                pl.BlockSpec(
                    (per_step, block, width), lambda i, s, m: (jnp.minimum(i, half - 1), 0, 0)
                ),
                pl.BlockSpec(
                    (per_step, block, width), lambda i, s, m: (jnp.maximum(i - half, 0), 0, 0)
                ),
            ),
            scratch_shapes=[
                pltpu.VMEM((blocks, block, width), BF16),
                pltpu.SemaphoreType.DMA((count,)),
            ],
        ),
        cost_estimate=cost(
            4 * tiles * slots * block * block * width,
            4 * tiles * slots * block * block + 2 * blocks * block * width,
        ),
        name="pixel_pass",
    )(ids, meta, *[gains] * STREAMS, *sources)


def whole(shape):
    return pl.BlockSpec(shape, lambda *_: (0,) * len(shape))


def share_kernel(mine, theirs, total, coded, *, groups):
    v = mine[...] + theirs[...]
    total[...] = v
    tiles, block, width = v.shape
    encode(v.reshape(tiles * block // SUB, SUB, width), coded, groups)


def share(mine, theirs):
    tiles, block, width = mine.shape
    per = PART * SUB * 2 // block
    parts, n = tiles // per, per * block // SUB
    part = pl.BlockSpec((per, block, width), lambda i: (i, 0, 0))
    return pl.pallas_call(
        functools.partial(share_kernel, groups=SUB),
        out_shape=(
            jax.ShapeDtypeStruct(mine.shape, F32),
            jax.ShapeDtypeStruct((parts * (n + 1), SUB, width), S16),
        ),
        grid=(parts,),
        in_specs=[part, part],
        out_specs=(part, pl.BlockSpec((n + 1, SUB, width), lambda i: (i, 0, 0))),
        cost_estimate=cost(mine.size * 8, mine.size * 14),
        compiler_params=ROOM,
        name="share",
    )(mine, theirs)


def finish_kernel(total, coded, out, *, groups):
    tiles, block, width = total.shape
    v = total[...] + decode(coded, groups).reshape(tiles, block, width)
    out[...] = v.astype(BF16)


def finish(total, coded):
    tiles, block, width = total.shape
    per = PART * SUB * 2 // block
    parts, n = tiles // per, per * block // SUB
    part = pl.BlockSpec((per, block, width), lambda i: (i, 0, 0))
    return pl.pallas_call(
        functools.partial(finish_kernel, groups=SUB),
        out_shape=jax.ShapeDtypeStruct(total.shape, BF16),
        grid=(parts,),
        in_specs=[part, pl.BlockSpec((n + 1, SUB, width), lambda i: (i, 0, 0))],
        out_specs=part,
        cost_estimate=cost(total.size * 4, total.size * 8),
        compiler_params=ROOM,
        name="finish",
    )(total, coded)


def beam_kernel(ids, meta, *refs, slots, per_step, half):
    streams = refs[:STREAMS]
    theirs, mine, out_ref = refs[STREAMS:]
    step = pl.program_id(0)

    @pl.when(step == 0)
    def _():
        out_ref[...] = jnp.zeros_like(out_ref)

    base = half_tiles(step, meta, half) * per_step * slots

    def sweep(source):
        for q in range(STREAMS):
            lax.fori_loop(0, streams[q].shape[0] // UNROLL, functools.partial(some, source, q), 0)

    def some(source, q, k, _):
            gains_ref = streams[q]
            for r in range(UNROLL):
                n = k * UNROLL + r
                i = q * gains_ref.shape[0] + n
                rows = source[i]
                for j in range(slots):
                    part = lax.dot_general(
                        gains_ref[n, j], rows, (((0,), (0,)), ((), ())), preferred_element_type=F32
                    )
                    out_ref[ids[base + i * slots + j]] += part
            return 0

    pl.when(step < half)(lambda: sweep(theirs))
    pl.when(step >= half)(lambda: sweep(mine))


def beam_pass(ids, meta, gains, theirs, mine, blocks):
    _, slots, block, _ = gains.shape
    tiles, _, width = mine.shape
    per_step = math.gcd(tiles, 16)
    half = tiles // per_step
    return pl.pallas_call(
        functools.partial(beam_kernel, slots=slots, per_step=per_step, half=half),
        out_shape=jax.ShapeDtypeStruct((blocks, block, width), F32),
        grid_spec=pltpu.PrefetchScalarGridSpec(
            num_scalar_prefetch=2,
            grid=(2 * half,),
            in_specs=gains_specs(per_step, slots, block, half)
            + [
                pl.BlockSpec(
                    (per_step, block, width), lambda i, s, m: (jnp.minimum(i, half - 1), 0, 0)
                ),
                pl.BlockSpec(
                    (per_step, block, width), lambda i, s, m: (jnp.maximum(i - half, 0), 0, 0)
                ),
            ],
            out_specs=pl.BlockSpec((blocks, block, width), lambda i, s, m: (0, 0, 0)),
        ),
        cost_estimate=cost(
            4 * tiles * slots * block * block * width,
            4 * tiles * slots * block * block + 4 * blocks * block * width,
        ),
        compiler_params=ROOM,
        name="beam_pass",
    )(ids, meta, *[gains] * STREAMS, theirs, mine)


def own_spec(sums, part, first, where):
    width = sums.shape[-1]
    if sums.ndim == 3:
        return pl.BlockSpec((part, SUB, width), lambda i, m: (first + i, m[1 + where], 0))
    return pl.BlockSpec((None, part, SUB, width), lambda i, m: (m[1 + where], first + i, 0, 0))


def part_spec(rows, width):
    return pl.BlockSpec((rows, SUB, width), lambda i, m: (i, 0, 0))


def hop_kernel(meta, *refs, arrivals, groups):
    ins, outs = list(refs[: -len(arrivals)]), refs[-len(arrivals) :]
    for came, out in zip(arrivals, outs):
        v = ins.pop(0)[...]
        if came:
            v = v + decode(ins.pop(0), groups)
        encode(v, out, groups)


def hop(meta, sums, places, first, tiles, arrivals):
    width = sums.shape[-1]
    part = math.gcd(tiles, PART)
    parts = tiles // part
    operands, specs = [], []
    for where, message in zip(places, arrivals):
        operands.append(sums)
        specs.append(own_spec(sums, part, first // part, where))
        if message is not None:
            operands.append(message)
            specs.append(part_spec(part + 1, width))
    shape = jax.ShapeDtypeStruct((parts * (part + 1), SUB, width), S16)
    size = tiles * SUB * width * len(arrivals)
    return pl.pallas_call(
        functools.partial(
            hop_kernel,
            arrivals=[m is not None for m in arrivals],
            groups=math.gcd(part, SUB),
        ),
        out_shape=[shape] * len(arrivals),
        grid_spec=pltpu.PrefetchScalarGridSpec(
            num_scalar_prefetch=1,
            grid=(parts,),
            in_specs=specs,
            out_specs=[part_spec(part + 1, width)] * len(arrivals),
        ),
        cost_estimate=cost(size * 6, size * 8),
        compiler_params=ROOM,
        name="hop",
    )(meta, *operands)


def last_kernel(meta, *refs, count, groups, earlier, chained):
    v = refs[0][...]
    for m in refs[1 : 1 + count]:
        v = v + decode(m, groups)
    flat = v.reshape(-1, v.shape[-1])
    out, gram = refs[-2:]
    out[...] = flat

    @pl.when(pl.program_id(0) == 0)
    def _():
        gram[...] = refs[-3][...] if chained else jnp.zeros_like(gram)

    def inner_products(a, b):
        return lax.dot_general(
            a, b, (((0,), (0,)), ((), ())), precision=HIGHEST, preferred_element_type=F32
        )

    if earlier:
        gram[0] += inner_products(refs[1 + count][...], flat)
    gram[gram.shape[0] - 1] += inner_products(flat, flat)


def last(meta, sums, first, tiles, arrivals, before, gram):
    width = sums.shape[-1]
    part = math.gcd(tiles, PART)
    parts, rows = tiles // part, part * SUB
    operands = [sums, *arrivals]
    specs = [own_spec(sums, part, first // part, 0)]
    specs += [part_spec(part + 1, width)] * len(arrivals)
    if before is not None:
        operands.append(before)
        specs.append(pl.BlockSpec((rows, width), lambda i, m: (first // part + i, 0)))
    grams = 1 if before is None else 2
    if gram is not None:
        operands.append(gram)
        specs.append(whole(gram.shape))
    return pl.pallas_call(
        functools.partial(
            last_kernel,
            count=len(arrivals),
            groups=math.gcd(part, SUB),
            earlier=before is not None,
            chained=gram is not None,
        ),
        out_shape=(
            jax.ShapeDtypeStruct((tiles * SUB, width), F32),
            jax.ShapeDtypeStruct((grams, width, width), F32),
        ),
        grid_spec=pltpu.PrefetchScalarGridSpec(
            num_scalar_prefetch=1,
            grid=(parts,),
            in_specs=specs,
            out_specs=[pl.BlockSpec((rows, width), lambda i, m: (i, 0)), whole((grams, width, width))],
        ),
        cost_estimate=cost(12 * grams * tiles * SUB * width * width, tiles * SUB * width * 12),
        compiler_params=ROOM,
        name="last",
    )(meta, *operands)


def product(a, b):
    return jnp.dot(a, b, precision=HIGHEST, preferred_element_type=F32)


PANEL = 16


def upper_factor(work):
    n = work.shape[0]
    below = lax.broadcasted_iota(jnp.int32, (PANEL, n), 0)

    def along(x, j):
        return jnp.broadcast_to(x[j : j + 1, :], (PANEL, n))

    for p in range(0, n, PANEL):
        rows = work[p : p + PANEL, :]
        spread = [jnp.broadcast_to(rows[:, p + k : p + k + 1], (PANEL, n)) for k in range(PANEL)]
        for j in range(PANEL):
            pivot = along(spread[j], j)
            root = lax.rsqrt(pivot)
            root = root * (1.5 - 0.5 * pivot * root * root)
            share_of = jnp.where(below > j, spread[j] * (root * root), 0.0)
            for k in range(j + 1, PANEL):
                spread[k] = spread[k] - share_of * along(spread[k], j)
            top = along(rows, j)
            rows = jnp.where(below == j, top * root, rows - share_of * top)
        work[p : p + PANEL, :] = rows
        if p + PANEL < n:
            update = lax.dot_general(
                rows, rows, (((0,), (0,)), ((), ())), precision=HIGHEST, preferred_element_type=F32
            )
            work[p + PANEL :, :] -= update[p + PANEL :, :]
    row = lax.broadcasted_iota(jnp.int32, (n, n), 0)
    column = lax.broadcasted_iota(jnp.int32, (n, n), 1)
    return jnp.where(row <= column, work[...], 0.0)


def inverse_of(upper):
    n = upper.shape[0]
    row = lax.broadcasted_iota(jnp.int32, (n, n), 0)
    column = lax.broadcasted_iota(jnp.int32, (n, n), 1)
    unit = jnp.where(row == column, 1.0, 0.0).astype(F32)
    diagonal = jnp.sum(upper * unit, axis=0, keepdims=True)
    scaled = upper / diagonal
    size = 8
    off = jnp.where(row // size == column // size, unit - scaled, 0.0)
    inverse = unit + off
    power = off
    for _ in range(2):
        power = product(power, power)
        inverse = inverse + product(inverse, power)
    while size < n:
        pair = (row // (2 * size) == column // (2 * size)) & (row // size != column // size)
        cross = jnp.where(pair, scaled, 0.0)
        inverse = inverse - product(product(inverse, cross), inverse)
        size *= 2
    return inverse / jnp.sum(unit * diagonal, axis=1, keepdims=True)


def first_kernel(*refs, count):
    gram, out, upper, inverse, work = refs[count:]
    rows = refs[0].shape[0]
    work[...] = gram[0]
    upper[...] = upper_factor(work)
    inverse[...] = inverse_of(upper[...])
    right = inverse[...]
    for p in range(count):
        out[pl.ds(p * rows, rows), :] = product(refs[p][...], right)


def apply_first(pieces, gram):
    rows, width = pieces[0].shape
    n = len(pieces)
    square = jax.ShapeDtypeStruct((width, width), F32)
    return pl.pallas_call(
        functools.partial(first_kernel, count=n),
        out_shape=(jax.ShapeDtypeStruct((rows * n, width), F32), square, square),
        scratch_shapes=[pltpu.VMEM((width, width), F32)],
        cost_estimate=cost(12 * n * rows * width * width, 8 * n * rows * width),
        compiler_params=ROOM,
        name="apply_first",
    )(*pieces, gram)


def basis_kernel(*refs, count, scale):
    first, upper, inverse, gram, basis, factor, work = refs[count:]
    rows, width = refs[0].shape
    low, high = slice(0, width), slice(width, 2 * width)
    cross = lax.dot_general(
        inverse[...], gram[0], (((0,), (0,)), ((), ())), precision=HIGHEST, preferred_element_type=F32
    )
    work[...] = gram[1] - lax.dot_general(
        cross, cross, (((0,), (0,)), ((), ())), precision=HIGHEST, preferred_element_type=F32
    )
    last_upper = upper_factor(work)
    factor[low, low] = upper[...] / scale
    factor[low, high] = cross / scale
    factor[high, low] = jnp.zeros_like(cross)
    factor[high, high] = last_upper / scale
    right = inverse_of(last_upper)
    for p in range(count):
        at = pl.ds(p * rows, rows)
        q = first[at, :]
        basis[at, low] = q * scale
        basis[at, high] = product(refs[p][...] - product(q, cross), right) * scale


def apply_both(pieces, first, upper, inverse, gram, scale):
    rows, width = pieces[0].shape
    n = len(pieces)
    return pl.pallas_call(
        functools.partial(basis_kernel, count=n, scale=scale),
        out_shape=(
            jax.ShapeDtypeStruct((rows * n, 2 * width), F32),
            jax.ShapeDtypeStruct((2 * width, 2 * width), F32),
        ),
        scratch_shapes=[pltpu.VMEM((width, width), F32)],
        cost_estimate=cost(24 * n * rows * width * width, 16 * n * rows * width),
        compiler_params=ROOM,
        name="apply_both",
    )(*pieces, first, upper, inverse, gram)


def plan_of(far):
    def gather(c, h):
        return [("ag", c, h, s) for s in range(GATHER_PIECES[c])]

    def scatter(c, h, s):
        return [("hop", c, h, s), ("rs", c, h, s)]

    plan = [item for h in range(far) for item in gather(0, h)] + gather(1, 0)
    plan += [("k1", 0), ("swap", 0)] + gather(1, 1) + [("share", 0), ("y", 0)]
    for h in range(2, far):
        plan += gather(1, h)
    plan += [("fin", 0), ("core", 0), ("k4", 0)]

    def first(h):
        return [item for s in range(SCATTER_PIECES[0]) for item in scatter(0, h, s)]

    plan += first(0) + [("k1", 1), ("swap", 1)] + first(1) + [("share", 1), ("y", 1)]
    for h in range(2, far - 1):
        plan += first(h)
    plan += [("fin", 1), ("core", 1)] + first(far - 1) + [("k4", 1)]
    for h in range(far):
        plan += [item for s in range(SCATTER_PIECES[1]) for item in scatter(1, h, s)]
        if h == 0:
            plan += [("last", 0, p) for p in range(SCATTER_PIECES[0])]
            plan += [("ar", 0, k) for k in range(3)]
        elif h < far - 1:
            plan += [("ar", 0, h + 2)]
    plan += [("first", 0)] + [("last", 1, s) for s in range(SCATTER_PIECES[1])]
    return plan


def solution(mesh):
    n_pix, n_beam = mesh.shape["pix"], mesh.shape["beam"]
    cycle = list(range(0, n_pix, 2)) + list(range(1, n_pix, 2))[::-1]
    onward = [(cycle[i], cycle[(i + 1) % n_pix]) for i in range(n_pix)]
    backward = [(b, a) for a, b in onward]
    inner = [(b, b ^ 1) for b in range(n_beam)]
    outer = [(b, b ^ 2) for b in range(n_beam)]
    table = np.zeros((n_pix * n_beam, 1 + n_pix), np.int32)
    for p in range(n_pix):
        around = [cycle[(cycle.index(p) + r) % n_pix] for r in range(n_pix)]
        for b in range(n_beam):
            table[p * n_beam + b] = [b % 2] + around
    most = n_pix // 2
    hops = [(most, n_pix - 1 - most), (n_pix - 1 - most, most)]
    strides = [(a, 2**k) for a, n in (("beam", n_beam), ("pix", n_pix)) for k in range(n.bit_length() - 1)]
    plan = plan_of(most)

    def local(sketch, gains, coverage):
        blocks, rows, columns = sketch.shape
        block = gains.shape[2]
        beams = blocks * n_beam * block
        width = columns // 2
        aligned = rows == SUB
        ids = coverage.reshape(-1)
        device = lax.axis_index("pix") * n_beam + lax.axis_index("beam")
        meta = lax.dynamic_index_in_dim(jnp.asarray(table), device, keepdims=False)
        tiles_here = blocks * rows // SUB
        own = {}
        for c in (0, 1):
            number = blocks // GATHER_PIECES[c]
            for p in range(GATHER_PIECES[c]):
                own[c, p] = sketch[p * number : (p + 1) * number, :, c * width : (c + 1) * width]
        flow, held = {}, {}

        def sources_of(c):
            sources, spans = [], []
            per_piece = blocks // GATHER_PIECES[c]
            for s in range(GATHER_PIECES[c]):
                offsets = {0: own[c, s]}
                for (d, h), x in sorted(flow["ag", c, s].items()):
                    offsets[(n_pix - h - 1) if d == 0 else (h + 1)] = x
                if aligned:
                    for r in sorted(offsets):
                        sources.append(offsets[r])
                        spans.append((s * per_piece, per_piece, r))
                else:
                    stack = jnp.stack([offsets[r] for r in range(n_pix)])
                    stack = stack[jnp.argsort(meta[1:])]
                    stack = stack.transpose(1, 0, 2, 3).reshape(per_piece, block, width)
                    sources.append(stack)
                    spans.append((s * per_piece, per_piece, None))
            return sources, spans

        def partials_of(x):
            if aligned:
                return x
            x = x.reshape(blocks, n_pix, rows, width).transpose(1, 0, 2, 3)
            return x.reshape(n_pix, blocks * rows // SUB, SUB, width)

        def passed(g, k):
            axis, stride = strides[k]
            return lax.ppermute(g, axis, [(b, b ^ stride) for b in range(mesh.shape[axis])])

        def run(item):
            kind, c = item[0], item[1] if len(item) > 1 else None
            if kind == "ag":
                _, _, h, s = item
                flows = flow.setdefault(("ag", c, s), {})
                for d, ring in enumerate((onward, backward)):
                    if h < hops[c][d]:
                        before = own[c, s] if h == 0 else flows[d, h - 1]
                        flows[d, h] = lax.ppermute(before, "pix", ring)
            elif kind == "k1":
                sources, spans = sources_of(c)
                held["away", c], held["kept", c] = pixel_pass(
                    ids, meta, gains, sources, spans, rows if aligned else block, blocks, width
                )
            elif kind == "swap":
                held["away", c] = lax.ppermute(held["away", c], "beam", inner)
            elif kind == "share":
                held["total", c], held["coded", c] = share(held["kept", c], held["away", c])
            elif kind == "y":
                held["came", c] = lax.ppermute(held["coded", c], "beam", outer)
            elif kind == "fin":
                held["zb", c] = finish(held["total", c], held["came", c])
            elif kind == "core":
                held["peer", c] = lax.ppermute(held["zb", c], "beam", inner)
            elif kind == "k4":
                sums = beam_pass(ids, meta, gains, held["peer", c], held["zb", c], blocks)
                held["sums", c] = partials_of(sums)
            elif kind == "hop":
                _, _, h, s = item
                live = [d for d in (0, 1) if h >= most - hops[c][d]]
                left = most - h
                places = [left if d == 0 else n_pix - left for d in live]
                came = [None if h == most - hops[c][d] else flow["rs", c, s, d] for d in live]
                tiles = tiles_here // SCATTER_PIECES[c]
                sent = hop(meta, held["sums", c], places, s * tiles, tiles, came)
                for d, message in zip(live, sent):
                    held["sent", c, s, d] = message
            elif kind == "rs":
                _, _, h, s = item
                for d, ring in enumerate((onward, backward)):
                    if h >= most - hops[c][d]:
                        flow["rs", c, s, d] = lax.ppermute(held["sent", c, s, d], "pix", ring)
            elif kind == "last":
                s = item[2]
                came = [flow["rs", c, s, d] for d in (0, 1) if ("rs", c, s, d) in flow]
                tiles = tiles_here // SCATTER_PIECES[c]
                held["y", c, s], held["gram", c] = last(
                    meta,
                    held["sums", c],
                    s * tiles,
                    tiles,
                    came,
                    held["y", 0, 0] if c else None,
                    held.get(("gram", c)),
                )
            elif kind == "ar" and item[2] < len(strides):
                held["gram", c] = held["gram", c] + passed(held["gram", c], item[2])
                held["stage", c] = item[2] + 1
            elif kind == "first":
                g = held["gram", c]
                for k in range(held["stage", c], len(strides)):
                    g = g + passed(g, k)
                held["q"], held["upper"], held["inverse"] = apply_first([held["y", 0, 0]], g)

        for item in plan:
            run(item)
        gram = held["gram", 1]
        for k in range(len(strides)):
            gram = gram + passed(gram, k)
        pieces = [held["y", 1, s] for s in range(SCATTER_PIECES[1])]
        scale = math.sqrt(float(beams))
        basis, factor = apply_both(pieces, held["q"], held["upper"], held["inverse"], gram, scale)
        return basis.reshape(blocks, rows, columns), factor

    return jax.shard_map(
        local,
        mesh=mesh,
        in_specs=(P("beam", "pix", None), P("pix", "beam", None, None), P("pix", "beam")),
        out_specs=(P("beam", "pix", None), P()),
        check_vma=False,
    )
```
